512 devices in a mesh: pipe: 8 (over x, y_hi), dp: 64 (over z, y_lo, core).
Axes of the slice: x: 4, y: 4 (y_hi: 2, y_lo: 2; y = y_hi * 2 + y_lo), z: 16, core: 2. Of those that a mesh axis runs over, the one named last changes fastest.
Arguments:
- saved: bfloat16 [8, 2, 64, 128, 1536], P('pipe', None, 'dp'), may hold values from -6 to 6
- out_grad: bfloat16 [2, 64, 128, 1536], P(None, 'dp'), may hold values from -16 to 16
- lengths: int32 [2, 64], P(None, 'dp'), may hold values from 1 to 128, 5120 in all within a row
- kernel: bfloat16 [8, 31, 1536], P('pipe'), may hold values from -1 to 1
- gain: float32 [8, 1536], P('pipe'), may hold values from 0.5 to 1.5
- bias: float32 [8, 1536], P('pipe'), may hold values from -3 to 3
Outputs:
- in_grads: bfloat16 [8, 2, 64, 128, 1536], P('pipe', None, 'dp')
- kernel_grad: float32 [8, 31, 1536], P('pipe', None, 'dp')
- gain_grad: float32 [8, 1536], P('pipe', 'dp')
- bias_grad: float32 [8, 1536], P('pipe', 'dp')
The draws below stay inside these ranges and needn't reach their ends.
Inputs may be any that keep to these rules, and one draw needn't show every extreme that they name: In every micro-batch the lengths sum to 64 * 128 * 5 // 8 and one reaches 128.
All inputs are finite; a program needn't handle non-finite values. No bound on the sum of `lengths` on one device may be relied on, other than what follows from the above.
Results may differ from the reference program's by a relative error of at most 0.0079.
Values may be sent and summed in bfloat16 or wider, within the bound.
No kernel may reach another device: no remote copies, remote signals or barrier semaphores. Data moves between devices by JAX's collectives and lax.ppermute only.
A program may use at most 64 MiB of HBM per device.

```python
import math
import jax
import jax.numpy as jnp
import numpy as np
from jax import lax

C = 1536
KW = 31
FR = 128
MB = 2
BATCH = 64
N_PIPE = 8


def raised(entries, own_key, source, target, shards_of, factor):
    def block_of(dim):
        return (jnp.arange(entries.shape[dim]) // (entries.shape[dim] // shards_of)).reshape((-1,) + (1,) * (entries.ndim - 1 - dim))

    near = jax.random.permutation(own_key, shards_of)[block_of(target)]
    far = (block_of(target) + shards_of // 2) % shards_of
    return jnp.where((block_of(source) == near) | (block_of(source) == far), factor * entries, entries)


def block_levels(rng, shape, shards, smallest, top_value):
    def one(axis_at, parts):
        heights = jax.random.uniform(jax.random.fold_in(jax.random.fold_in(rng, 6), axis_at), (parts,), jnp.float32, smallest / len(shards), top_value / len(shards))
        return jnp.repeat(jnp.exp(heights), shape[axis_at] // parts).reshape((-1,) + (1,) * (len(shape) - axis_at - 1))

    level = one(*shards[0])
    for cut in shards[1:]:
        level = level * one(*cut)
    return level


def split_up(amount, total, reach, skew):
    weights = [(1 << 20) // math.isqrt(grade ** skew) + 1 for grade in range(2, amount + 1)]
    spare, given = total - reach - (amount - 1), [1] * (amount - 1)
    while spare > 0:
        movable = [i for i in range(amount - 1) if given[i] < reach]
        pool, left = sum([weights[i] for i in movable]), spare
        for i in movable:
            addition = min(reach - given[i], max(1, left * weights[i] // pool), spare)
            given[i] = given[i] + addition
            spare = spare - addition
    return np.array([reach] + given)


def ragged_sizes(rng, amount, total, most, slope):
    if amount == 2:
        one = jax.random.randint(rng, (), max(1, total - most), min(most, total - 1) + 1)
        return jnp.stack([one, total - one])
    tallies = jnp.asarray(split_up(amount, total, most, slope), jnp.int32)
    pairs = (amount - 1) // 2
    giver, taker = tallies[1:1 + 2 * pairs:2], tallies[2:2 + 2 * pairs:2]
    margin = jnp.minimum(giver - 1, most - taker)
    passed = jax.random.randint(jax.random.fold_in(rng, 1), (pairs,), 0, 1 << 20) % (margin + 1)
    tallies = tallies.at[1:1 + 2 * pairs:2].set(giver - passed).at[2:2 + 2 * pairs:2].set(taker + passed)
    return tallies[jax.random.permutation(jax.random.fold_in(rng, 2), amount)]


def noise(stream_key, extent, deviation, reach, cuts=(), kind=jnp.bfloat16):
    level = block_levels(stream_key, extent, cuts, -0.22, 0.18) if cuts else 1.0
    result = jax.random.normal(stream_key, extent, jnp.float32) * deviation * level
    return jnp.minimum(jnp.maximum(result, -reach), reach).astype(kind)


def bell_draw_with(rng, shape, scale, most, split, heavy, kind=jnp.bfloat16):
    result = scale * jax.random.normal(rng, shape, jnp.float32)
    if split:
        result = result * block_levels(rng, shape, split, -0.22, 0.18)
    return jnp.clip(raised(result, jax.random.fold_in(rng, 3), *heavy), -most, most).astype(kind)


def setup_inputs(seed: int = 0) -> dict:
    key_of = jax.random.split(jax.random.key(seed), 7)
    return {
        "saved": noise(key_of[0], (N_PIPE, MB, BATCH, FR, C), 1.0, 6.0, ((0, 8), (2, 64))),
        "out_grad": bell_draw_with(key_of[1], (MB, BATCH, FR, C), 1.0, 16.0, ((1, 64),), (1, 3, 64, 4.0)),
        "lengths": jax.vmap(lambda own: ragged_sizes(own, BATCH, BATCH * FR * 5 // 8, FR, 0))(jax.random.split(key_of[2], MB)).reshape((MB, BATCH)).astype(jnp.int32),
        "kernel": noise(key_of[3], (N_PIPE, KW, C), KW ** -0.5, 1.0, ((0, 8),)),
        "gain": jnp.clip(1.0 + 0.1 * jax.random.normal(key_of[4], (N_PIPE, C), jnp.float32), 0.5, 1.5),
        "bias": noise(key_of[5], (N_PIPE, C), 0.5, 3.0, ((0, 8),), jnp.float32),
    }


def backward_frames(x, dy, length, kernel, gain, bias):
    frames = x.shape[0]
    half = (KW - 1) // 2
    mask = (jnp.arange(frames, dtype=jnp.int32) < length)[:, None]
    weights = kernel.astype(jnp.float32)
    xm = jnp.where(mask, x.astype(jnp.float32), jnp.zeros((), jnp.float32))
    padded = jnp.pad(xm, ((half, half), (0, 0)))
    h = jnp.zeros_like(xm)
    for j in range(KW):
        h = h + weights[j] * padded[j:j + frames]
    mu = lax.optimization_barrier(jnp.mean(h, -1, keepdims=True))
    centred = h - mu
    recip = lax.rsqrt(lax.optimization_barrier(jnp.mean(centred * centred, -1, keepdims=True)) + 1e-05)
    normed = centred * recip
    u = normed * gain + bias
    incoming = dy.astype(jnp.float32)
    dv = jnp.where(mask, incoming, jnp.zeros((), jnp.float32))
    sig = jax.nn.sigmoid(u)
    du = dv * sig * (1.0 + u * (1.0 - sig))
    dnorm = du * gain
    dh = recip * (dnorm - lax.optimization_barrier(jnp.mean(dnorm, -1, keepdims=True)) - normed * lax.optimization_barrier(jnp.mean(dnorm * normed, -1, keepdims=True)))
    kgrad = jnp.stack([lax.optimization_barrier(jnp.sum(dh * padded[j:j + frames], 0)) for j in range(KW)], 0)
    dpad = jnp.pad(dh, ((half, half), (0, 0)))
    back = jnp.zeros_like(xm)
    for j in range(KW):
        back = back + weights[j] * dpad[KW - 1 - j:KW - 1 - j + frames]
    dx = jnp.where(mask, incoming + back, jnp.zeros((), jnp.float32)).astype(jnp.bfloat16)
    return (dx, kgrad, lax.optimization_barrier(jnp.sum(du * normed, 0)), lax.optimization_barrier(jnp.sum(du, 0)))

def reference(saved, out_grad, lengths, kernel, gain, bias):
    sections = saved.shape[0]
    shape = out_grad.shape
    items = shape[0] * shape[1]
    incoming = out_grad.reshape((items, shape[2], shape[3]))
    flat_lengths = lengths.reshape((items,)).astype(jnp.int32)
    grads_list, kernel_list, gain_list, bias_list = ([], [], [], [])
    for section in range(sections - 1, -1, -1):
        inputs = saved[section].reshape((items, shape[2], shape[3]))

        def single(operands):
            return backward_frames(operands[0], operands[1], operands[2], kernel[section], gain[section], bias[section])
        dx, kgrads, gsums, bsums = lax.map(single, (inputs, incoming, flat_lengths))
        grads_list.append(dx.reshape(shape))
        kernel_list.append(lax.optimization_barrier(jnp.sum(kgrads, 0)))
        gain_list.append(lax.optimization_barrier(jnp.sum(gsums, 0)))
        bias_list.append(lax.optimization_barrier(jnp.sum(bsums, 0)))
        incoming = dx
    grads_list = grads_list[::-1]
    kernel_list = kernel_list[::-1]
    gain_list = gain_list[::-1]
    bias_list = bias_list[::-1]
    return (jnp.stack(grads_list, 0), jnp.stack(kernel_list, 0), jnp.stack(gain_list, 0), jnp.stack(bias_list, 0))
```

```python
import functools
import jax
import jax.numpy as jnp
from jax import lax
from jax.experimental import pallas as pl
from jax.experimental.pallas import tpu as pltpu
from jax.sharding import PartitionSpec as P

KW = 31
HALF = 15
LANES = 128
LEAD = 16
PADDED = 160
EPS = 1e-05
F32 = jnp.float32
BF16 = jnp.bfloat16
VMEM = pl.BlockSpec(memory_space=pltpu.VMEM)
SMEM = pl.BlockSpec(memory_space=pltpu.SMEM)
ANY = pl.BlockSpec(memory_space=pl.ANY)


def columns(block):
    return pl.ds(pl.multiple_of(block * LANES, LANES), LANES)


def row_mean(partial, width):
    return jnp.broadcast_to(jnp.sum(partial, 1, keepdims=True) * (1.0 / width), partial.shape)


def live(length, frames):
    return lax.broadcasted_iota(jnp.int32, (frames, LANES), 0) < length


def clear_margins(pad_ref, frames):
    pad_ref[:, 0:LEAD, :] = jnp.zeros((pad_ref.shape[0], LEAD, LANES), F32)
    tail = PADDED - LEAD - frames
    pad_ref[:, LEAD + frames :, :] = jnp.zeros((pad_ref.shape[0], tail, LANES), F32)


def forward_kernel(len_ref, x_ref, w_ref, s_ref, pad_ref):
    frames, width = x_ref.shape
    blocks = width // LANES
    mask = live(len_ref[0], frames)
    clear_margins(pad_ref, frames)
    zero = jnp.zeros((frames, LANES), F32)

    def convolve(b, total):
        cols = columns(b)
        pad_ref[b, LEAD : LEAD + frames, :] = jnp.where(mask, x_ref[:, cols].astype(F32), 0.0)
        h = zero
        for j in range(KW):
            h = h + w_ref[j : j + 1, cols] * pad_ref[b, LEAD - HALF + j : LEAD - HALF + j + frames, :]
        s_ref[b] = h
        return total + h

    mu = row_mean(lax.fori_loop(0, blocks, convolve, zero), width)

    def square(b, total):
        centred = s_ref[b] - mu
        return total + centred * centred

    recip = lax.rsqrt(row_mean(lax.fori_loop(0, blocks, square, zero), width) + EPS)
    s_ref[2 * blocks] = recip

    def activate(b, carry):
        cols = columns(b)
        normed = (s_ref[b] - mu) * recip
        u = normed * w_ref[KW : KW + 1, cols] + w_ref[KW + 1 : KW + 2, cols]
        sig = jax.nn.sigmoid(u)
        s_ref[b] = normed
        s_ref[blocks + b] = jnp.where(mask, sig * (1.0 + u * (1.0 - sig)), 0.0)
        return carry

    lax.fori_loop(0, blocks, activate, 0)


def forward(length, x, w, limit=16 << 20):
    frames, width = x.shape
    blocks = width // LANES
    return pl.pallas_call(
        forward_kernel,
        out_shape=jax.ShapeDtypeStruct((2 * blocks + 1, frames, LANES), F32),
        in_specs=[SMEM, VMEM, VMEM],
        out_specs=VMEM,
        scratch_shapes=[pltpu.VMEM((blocks, PADDED, LANES), F32)],
        compiler_params=pltpu.CompilerParams(vmem_limit_bytes=limit),
        cost_estimate=pl.CostEstimate(flops=frames * width * 100, bytes_accessed=3 << 20, transcendentals=frames * width),
        name="forward",
    )(length, x, w)


def section(i, mask, dy_ref, s_ref, w_ref, pad_ref, dx_ref, gb_ref, dh_ref):
    frames, width = dy_ref.shape
    blocks = width // LANES
    zero = jnp.zeros((frames, LANES), F32)

    def scale(b, totals):
        first, second = totals
        cols = columns(b)
        normed = s_ref[i, b]
        du = dy_ref[:, cols].astype(F32) * s_ref[i, blocks + b]
        dnorm = du * w_ref[i, KW : KW + 1, cols]
        pad_ref[b, LEAD : LEAD + frames, :] = dnorm
        if gb_ref is not None:
            gb_ref[i, 0:1, cols] = jnp.sum(du * normed, 0, keepdims=True)
            gb_ref[i, 1:2, cols] = jnp.sum(du, 0, keepdims=True)
        return first + dnorm, second + dnorm * normed

    first, second = lax.fori_loop(0, blocks, scale, (zero, zero))
    first, second = row_mean(first, width), row_mean(second, width)

    def convolve(b, carry):
        cols = columns(b)
        dh = s_ref[i, 2 * blocks] * (pad_ref[b, LEAD : LEAD + frames, :] - first - s_ref[i, b] * second)
        pad_ref[b, LEAD : LEAD + frames, :] = dh
        if dh_ref is not None:
            dh_ref[i, b] = dh
        back = dy_ref[:, cols].astype(F32)
        for j in range(KW):
            start = LEAD + HALF - j
            back = back + w_ref[i, j : j + 1, cols] * pad_ref[b, start : start + frames, :]
        dx_ref[:, cols] = jnp.where(mask, back, 0.0).astype(BF16)
        return carry

    lax.fori_loop(0, blocks, convolve, 0)


def phase_kernel(n_dy, last, info_ref, *refs):
    dys = refs[:n_dy]
    s_local, s_other, w_local, w_other = refs[n_dy : n_dy + 4]
    refs = refs[n_dy + 4 :]
    if last:
        own_ref, give_ref, gb_ref, dh_ref = refs[:4]
        dy_ref, first_ref, s_ref, w_ref, pad_ref, sem, dx_ref = refs[4:]
    else:
        dx_ref = refs[0]
        dy_ref, first_ref, s_ref, w_ref, pad_ref, sem = refs[1:]
        gb_ref = dh_ref = None
    length, stage, local_first = info_ref[0], info_ref[1], info_ref[2]
    frames = dy_ref.shape[0]

    def fetch(a, b):
        return [
            pltpu.make_async_copy(a[0], w_ref.at[0], sem.at[1]),
            pltpu.make_async_copy(a[1], s_ref.at[0], sem.at[2]),
            pltpu.make_async_copy(b[0], w_ref.at[1], sem.at[3]),
            pltpu.make_async_copy(b[1], s_ref.at[1], sem.at[4]),
        ]

    chosen = jnp.minimum(stage, n_dy - 1)
    for k in range(n_dy):

        @pl.when(chosen == k)
        def _():
            pltpu.make_async_copy(dys[k], dy_ref, sem.at[0]).start()

    ahead = fetch((w_local, s_local), (w_other, s_other))
    behind = fetch((w_other, s_other), (w_local, s_local))

    @pl.when(local_first == 1)
    def _():
        for copy in ahead:
            copy.start()

    @pl.when(local_first != 1)
    def _():
        for copy in behind:
            copy.start()

    clear_margins(pad_ref, frames)
    mask = live(length, frames)
    pltpu.make_async_copy(dys[0], dy_ref, sem.at[0]).wait()
    ahead[0].wait()
    ahead[1].wait()
    section(0, mask, dy_ref, s_ref, w_ref, pad_ref, first_ref, gb_ref, dh_ref)
    ahead[2].wait()
    ahead[3].wait()
    section(1, mask, first_ref, s_ref, w_ref, pad_ref, dx_ref, gb_ref, dh_ref)
    if last:

        @pl.when(local_first == 1)
        def _():
            own_ref[...] = first_ref[...]
            give_ref[...] = dx_ref[...]

        @pl.when(local_first != 1)
        def _():
            own_ref[...] = dx_ref[...]
            give_ref[...] = first_ref[...]


def phase(info, dys, s_local, s_other, w_local, w_other, last, limit=20 << 20):
    frames, width = dys[0].shape
    blocks = width // LANES
    dx = jax.ShapeDtypeStruct((frames, width), BF16)
    out_shape = [dx]
    scratch = [
        pltpu.VMEM((frames, width), BF16),
        pltpu.VMEM((frames, width), BF16),
        pltpu.VMEM((2,) + s_local.shape, F32),
        pltpu.VMEM((2,) + w_local.shape, F32),
        pltpu.VMEM((blocks, PADDED, LANES), F32),
        pltpu.SemaphoreType.DMA((5,)),
    ]
    if last:
        out_shape = [
            dx,
            dx,
            jax.ShapeDtypeStruct((2, 8, width), F32),
            jax.ShapeDtypeStruct((2, blocks, frames, LANES), F32),
        ]
        scratch.append(pltpu.VMEM((frames, width), BF16))
    return pl.pallas_call(
        functools.partial(phase_kernel, len(dys), last),
        out_shape=out_shape,
        in_specs=[SMEM] + [ANY] * (len(dys) + 4),
        out_specs=[VMEM] * len(out_shape),
        scratch_shapes=scratch,
        compiler_params=pltpu.CompilerParams(vmem_limit_bytes=limit),
        cost_estimate=pl.CostEstimate(flops=frames * width * 160, bytes_accessed=5 << 20, transcendentals=0),
        name="phase_last" if last else "phase",
    )(info, *dys, s_local, s_other, w_local, w_other)


def kernel_grad_kernel(info_ref, x_ref, dh_ref, gb_ref, out_ref, pad_ref):
    frames, width = x_ref.shape
    blocks = width // LANES
    mask = live(info_ref[0], frames)
    clear_margins(pad_ref, frames)
    out_ref[KW + 2 :, :] = jnp.zeros((out_ref.shape[0] - KW - 2, width), out_ref.dtype)

    def correlate(b, carry):
        cols = columns(b)
        pad_ref[b, LEAD : LEAD + frames, :] = jnp.where(mask, x_ref[:, cols].astype(F32), 0.0)
        dh = dh_ref[0, b]
        rows = []
        for j in range(KW):
            product = dh * pad_ref[b, LEAD - HALF + j : LEAD - HALF + j + frames, :]
            rows.append(jnp.sum(product, 0, keepdims=True))
        rows.append(gb_ref[0, 0:1, cols])
        rows.append(gb_ref[0, 1:2, cols])
        out_ref[: KW + 2, cols] = jnp.concatenate(rows, 0).astype(out_ref.dtype)
        return carry

    lax.fori_loop(0, blocks, correlate, 0)


def kernel_grad(info, x, dh, gb, which, dtype, limit=16 << 20):
    frames, width = x.shape
    blocks = width // LANES
    return pl.pallas_call(
        kernel_grad_kernel,
        grid_spec=pltpu.PrefetchScalarGridSpec(
            num_scalar_prefetch=1,
            grid=(1,),
            in_specs=[
                pl.BlockSpec((frames, width), lambda i, s: (0, 0)),
                pl.BlockSpec((1, blocks, frames, LANES), lambda i, s: (s[which], 0, 0, 0)),
                pl.BlockSpec((1, 8, width), lambda i, s: (s[which], 0, 0)),
            ],
            out_specs=pl.BlockSpec((40, width), lambda i, s: (0, 0)),
            scratch_shapes=[pltpu.VMEM((blocks, PADDED, LANES), F32)],
        ),
        out_shape=jax.ShapeDtypeStruct((40, width), dtype),
        compiler_params=pltpu.CompilerParams(vmem_limit_bytes=limit),
        cost_estimate=pl.CostEstimate(flops=frames * width * 62, bytes_accessed=2 << 20, transcendentals=0),
        name="kernel_grad",
    )(info, x, dh, gb)


def pack_kernel(own_ref, other_ref, out_ref, turned_ref):
    rows, width = own_ref.shape
    filler = jnp.zeros((LANES - rows, LANES), F32)

    def turn(b, carry):
        cols = columns(b)
        total = own_ref[:, cols] + other_ref[:, cols].astype(F32)
        turned_ref[columns(b), :] = jnp.concatenate([total, filler], 0).T
        return carry

    lax.fori_loop(0, width // LANES, turn, 0)
    share = width // out_ref.shape[0]

    def gather(d, carry):
        start = pl.multiple_of(d * share, 8)
        packed = turned_ref[pl.ds(start, 8), :]
        for g in range(1, share // 8):
            packed = packed + pltpu.roll(turned_ref[pl.ds(start + 8 * g, 8), :], rows * g, 1)
        out_ref[d] = packed.astype(out_ref.dtype)
        return carry

    lax.fori_loop(0, out_ref.shape[0], gather, 0)


def pack(own, other, members, limit=8 << 20):
    width = own.shape[1]
    return pl.pallas_call(
        pack_kernel,
        out_shape=jax.ShapeDtypeStruct((members, 8, LANES), BF16),
        in_specs=[VMEM, VMEM],
        out_specs=VMEM,
        scratch_shapes=[pltpu.VMEM((width, LANES), F32)],
        compiler_params=pltpu.CompilerParams(vmem_limit_bytes=limit),
        name="pack",
    )(own, other)


def finish_kernel(rows, parts_ref, kernel_ref, gain_ref, bias_ref):
    share = kernel_ref.shape[1]
    total = jnp.sum(parts_ref[...].astype(F32), 0)
    turned = jnp.concatenate([total, jnp.zeros((LANES - 8, LANES), F32)], 0).T
    value = turned[:rows]
    for g in range(1, share // 8):
        value = value + pltpu.roll(turned[rows * g : rows * (g + 1)], 8 * g, 1)
    kernel_ref[...] = value[:KW, :share]
    gain_ref[...] = value[KW : KW + 1, :share]
    bias_ref[...] = value[KW + 1 : KW + 2, :share]


def finish(parts, rows, share, limit=8 << 20):
    return pl.pallas_call(
        functools.partial(finish_kernel, rows),
        out_shape=[
            jax.ShapeDtypeStruct((KW, share), F32),
            jax.ShapeDtypeStruct((1, share), F32),
            jax.ShapeDtypeStruct((1, share), F32),
        ],
        in_specs=[VMEM],
        out_specs=[VMEM, VMEM, VMEM],
        compiler_params=pltpu.CompilerParams(vmem_limit_bytes=limit),
        name="finish",
    )(parts)


def local(saved, out_grad, lengths, kernel, gain, bias):
    sections = lax.axis_size("pipe")
    members = lax.axis_size("dp")
    place = lax.axis_index("pipe")
    upper = place % 2
    item = 1 - upper
    stages = sections // 2
    stage = stages - 1 - place // 2
    swap = [(p, p ^ 1) for p in range(sections)]
    x_both = saved[0, :, 0]
    x_give = lax.dynamic_index_in_dim(x_both, 1 - item, 0, keepdims=False)
    x_local = lax.dynamic_index_in_dim(x_both, item, 0, keepdims=False)
    w_local = jnp.concatenate([kernel[0].astype(F32), gain, bias], 0)
    w_other = lax.ppermute(w_local, "pipe", swap)
    x_other = lax.ppermute(x_give, "pipe", swap)
    dys = [lax.dynamic_index_in_dim(out_grad[:, 0], item, 0, keepdims=False)]
    length = lax.dynamic_index_in_dim(lengths[:, 0], item, 0, keepdims=False)
    info = jnp.stack([length, stage, upper, 1 - upper, upper]).astype(jnp.int32)
    s_local = forward(info, x_local, w_local)
    s_other = forward(info, x_other, w_other)
    for k in range(stages - 1):
        (dx,) = phase(info, dys, s_local, s_other, w_local, w_other, False)
        top = sections - 1 - 2 * k
        dys.append(lax.ppermute(dx, "pipe", [(top, top - 2), (top - 1, top - 3)]))
    own, give, gb, dh = phase(info, dys, s_local, s_other, w_local, w_other, True)
    kg_give = kernel_grad(info, x_other, dh, gb, 4, BF16)
    kg_other = lax.ppermute(kg_give, "pipe", swap)
    dx_other = lax.ppermute(give, "pipe", swap)
    kg_own = kernel_grad(info, x_local, dh, gb, 3, F32)
    packed = pack(kg_own, kg_other, members)
    parts = lax.all_to_all(packed, "dp", 0, 0, tiled=True)
    kernel_part, gain_part, bias_part = finish(parts, kg_own.shape[0], kernel.shape[2] // members)
    grads = jnp.where(item == 0, jnp.stack([own, dx_other]), jnp.stack([dx_other, own]))
    return (grads[None, :, None], kernel_part[None], gain_part, bias_part)


def solution(mesh):
    return jax.shard_map(
        local,
        mesh=mesh,
        in_specs=(
            P("pipe", None, "dp", None, None),
            P(None, "dp", None, None),
            P(None, "dp"),
            P("pipe", None, None),
            P("pipe", None),
            P("pipe", None),
        ),
        out_specs=(
            P("pipe", None, "dp", None, None),
            P("pipe", None, "dp"),
            P("pipe", "dp"),
            P("pipe", "dp"),
        ),
        check_vma=False,
    )
```

```python
import functools
import jax
import jax.numpy as jnp
from jax import lax
from jax.experimental import pallas as pl
from jax.experimental.pallas import tpu as pltpu
from jax.sharding import PartitionSpec as P


KW = 31
HALF = 15
LANES = 128
LEAD = 16
PADDED = 160
EPS = 1e-05
ROWS = 40
F32 = jnp.float32
BF16 = jnp.bfloat16
VMEM = pl.BlockSpec(memory_space=pltpu.VMEM)
SMEM = pl.BlockSpec(memory_space=pltpu.SMEM)
ANY = pl.BlockSpec(memory_space=pl.ANY)


def columns(block):
    return pl.ds(pl.multiple_of(block * LANES, LANES), LANES)


def row_mean(partial, width):
    return jnp.broadcast_to(jnp.sum(partial, 1, keepdims=True) * (1.0 / width), partial.shape)


def live(length, frames):
    return lax.broadcasted_iota(jnp.int32, (frames, LANES), 0) < length


def clear_margins(pad_ref, frames):
    pad_ref[:, 0:LEAD, :] = jnp.zeros((pad_ref.shape[0], LEAD, LANES), F32)
    tail = PADDED - LEAD - frames
    pad_ref[:, LEAD + frames :, :] = jnp.zeros((pad_ref.shape[0], tail, LANES), F32)


def forward_kernel(len_ref, x_ref, w_ref, s_ref, pad_ref):
    frames, width = x_ref.shape
    blocks = width // LANES
    mask = live(len_ref[0], frames)
    clear_margins(pad_ref, frames)
    zero = jnp.zeros((frames, LANES), F32)

    def convolve(b, total):
        cols = columns(b)
        pad_ref[b, LEAD : LEAD + frames, :] = jnp.where(mask, x_ref[:, cols].astype(F32), 0.0)
        h = zero
        for j in range(KW):
            h = h + w_ref[j : j + 1, cols] * pad_ref[b, LEAD - HALF + j : LEAD - HALF + j + frames, :]
        s_ref[b] = h
        return total + h

    mu = row_mean(lax.fori_loop(0, blocks, convolve, zero), width)

    def square(b, total):
        centred = s_ref[b] - mu
        return total + centred * centred

    recip = lax.rsqrt(row_mean(lax.fori_loop(0, blocks, square, zero), width) + EPS)
    s_ref[2 * blocks] = recip

    def activate(b, carry):
        cols = columns(b)
        normed = (s_ref[b] - mu) * recip
        u = normed * w_ref[KW : KW + 1, cols] + w_ref[KW + 1 : KW + 2, cols]
        sig = jax.nn.sigmoid(u)
        s_ref[b] = normed
        s_ref[blocks + b] = jnp.where(mask, sig * (1.0 + u * (1.0 - sig)), 0.0)
        return carry

    lax.fori_loop(0, blocks, activate, 0)


def forward(length, x, w, limit=16 << 20):
    frames, width = x.shape
    blocks = width // LANES
    return pl.pallas_call(
        forward_kernel,
        out_shape=jax.ShapeDtypeStruct((2 * blocks + 1, frames, LANES), F32),
        in_specs=[SMEM, VMEM, VMEM],
        out_specs=VMEM,
        scratch_shapes=[pltpu.VMEM((blocks, PADDED, LANES), F32)],
        compiler_params=pltpu.CompilerParams(vmem_limit_bytes=limit),
        cost_estimate=pl.CostEstimate(flops=frames * width * 100, bytes_accessed=3 << 20, transcendentals=frames * width),
        name="forward",
    )(length, x, w)


def section(i, mask, dy_ref, s_ref, w_ref, pad_ref, dx_ref, gb_ref, dh_ref):
    frames, width = dy_ref.shape
    blocks = width // LANES
    zero = jnp.zeros((frames, LANES), F32)

    def scale(b, totals):
        first, second = totals
        cols = columns(b)
        normed = s_ref[i, b]
        du = dy_ref[:, cols].astype(F32) * s_ref[i, blocks + b]
        dnorm = du * w_ref[i, KW : KW + 1, cols]
        pad_ref[b, LEAD : LEAD + frames, :] = dnorm
        if gb_ref is not None:
            gb_ref[i, 0:1, cols] = jnp.sum(du * normed, 0, keepdims=True)
            gb_ref[i, 1:2, cols] = jnp.sum(du, 0, keepdims=True)
        return first + dnorm, second + dnorm * normed

    first, second = lax.fori_loop(0, blocks, scale, (zero, zero))
    first, second = row_mean(first, width), row_mean(second, width)

    def convolve(b, carry):
        cols = columns(b)
        dh = s_ref[i, 2 * blocks] * (pad_ref[b, LEAD : LEAD + frames, :] - first - s_ref[i, b] * second)
        pad_ref[b, LEAD : LEAD + frames, :] = dh
        if dh_ref is not None:
            dh_ref[i, b] = dh
        back = dy_ref[:, cols].astype(F32)
        for j in range(KW):
            start = LEAD + HALF - j
            back = back + w_ref[i, j : j + 1, cols] * pad_ref[b, start : start + frames, :]
        dx_ref[:, cols] = jnp.where(mask, back, 0.0).astype(BF16)
        return carry

    lax.fori_loop(0, blocks, convolve, 0)


def phase_kernel(n_dy, last, info_ref, *refs):
    dys = refs[:n_dy]
    s_local, s_other, w_local, w_other = refs[n_dy : n_dy + 4]
    refs = refs[n_dy + 4 :]
    if last:
        own_ref, give_ref, gb_ref, dh_ref = refs[:4]
        dy_ref, first_ref, s_ref, w_ref, pad_ref, sem, dx_ref = refs[4:]
    else:
        dx_ref = refs[0]
        dy_ref, first_ref, s_ref, w_ref, pad_ref, sem = refs[1:]
        gb_ref = dh_ref = None
    length, stage, local_first = info_ref[0], info_ref[1], info_ref[2]
    frames = dy_ref.shape[0]

    def fetch(a, b):
        return [
            pltpu.make_async_copy(a[0], w_ref.at[0], sem.at[1]),
            pltpu.make_async_copy(a[1], s_ref.at[0], sem.at[2]),
            pltpu.make_async_copy(b[0], w_ref.at[1], sem.at[3]),
            pltpu.make_async_copy(b[1], s_ref.at[1], sem.at[4]),
        ]

    chosen = jnp.minimum(stage, n_dy - 1)
    for k in range(n_dy):

        @pl.when(chosen == k)
        def _():
            pltpu.make_async_copy(dys[k], dy_ref, sem.at[0]).start()

    ahead = fetch((w_local, s_local), (w_other, s_other))
    behind = fetch((w_other, s_other), (w_local, s_local))

    @pl.when(local_first == 1)
    def _():
        for copy in ahead:
            copy.start()

    @pl.when(local_first != 1)
    def _():
        for copy in behind:
            copy.start()

    clear_margins(pad_ref, frames)
    mask = live(length, frames)
    pltpu.make_async_copy(dys[0], dy_ref, sem.at[0]).wait()
    ahead[0].wait()
    ahead[1].wait()
    section(0, mask, dy_ref, s_ref, w_ref, pad_ref, first_ref, gb_ref, dh_ref)
    ahead[2].wait()
    ahead[3].wait()
    section(1, mask, first_ref, s_ref, w_ref, pad_ref, dx_ref, gb_ref, dh_ref)
    if last:

        @pl.when(local_first == 1)
        def _():
            own_ref[...] = first_ref[...]
            give_ref[...] = dx_ref[...]

        @pl.when(local_first != 1)
        def _():
            own_ref[...] = dx_ref[...]
            give_ref[...] = first_ref[...]


def phase(info, dys, s_local, s_other, w_local, w_other, last, limit=20 << 20):
    frames, width = dys[0].shape
    blocks = width // LANES
    dx = jax.ShapeDtypeStruct((frames, width), BF16)
    out_shape = [dx]
    scratch = [
        pltpu.VMEM((frames, width), BF16),
        pltpu.VMEM((frames, width), BF16),
        pltpu.VMEM((2,) + s_local.shape, F32),
        pltpu.VMEM((2,) + w_local.shape, F32),
        pltpu.VMEM((blocks, PADDED, LANES), F32),
        pltpu.SemaphoreType.DMA((5,)),
    ]
    if last:
        out_shape = [
            dx,
            dx,
            jax.ShapeDtypeStruct((2, 8, width), F32),
            jax.ShapeDtypeStruct((2, blocks, frames, LANES), F32),
        ]
        scratch.append(pltpu.VMEM((frames, width), BF16))
    return pl.pallas_call(
        functools.partial(phase_kernel, len(dys), last),
        out_shape=out_shape,
        in_specs=[SMEM] + [ANY] * (len(dys) + 4),
        out_specs=[VMEM] * len(out_shape),
        scratch_shapes=scratch,
        compiler_params=pltpu.CompilerParams(vmem_limit_bytes=limit),
        cost_estimate=pl.CostEstimate(flops=frames * width * 160, bytes_accessed=5 << 20, transcendentals=0),
        name="phase_last" if last else "phase",
    )(info, *dys, s_local, s_other, w_local, w_other)


def kernel_grad_kernel(rows, info_ref, x_ref, dh_ref, gb_ref, out_ref, pad_ref, turned_ref):
    frames, width = x_ref.shape
    blocks = width // LANES
    members = out_ref.shape[0]
    share = width // members
    mask = live(info_ref[0], frames)
    clear_margins(pad_ref, frames)
    filler = jnp.zeros((LANES - KW - 2, LANES), F32)

    def correlate(b, carry):
        cols = columns(b)
        pad_ref[b, LEAD : LEAD + frames, :] = jnp.where(mask, x_ref[:, cols].astype(F32), 0.0)
        dh = dh_ref[0, b]
        sums = []
        for j in range(KW):
            product = dh * pad_ref[b, LEAD - HALF + j : LEAD - HALF + j + frames, :]
            sums.append(jnp.sum(product, 0, keepdims=True))
        sums.append(gb_ref[0, 0:1, cols])
        sums.append(gb_ref[0, 1:2, cols])
        turned_ref[cols, :] = jnp.concatenate(sums + [filler], 0).T
        return carry

    lax.fori_loop(0, blocks, correlate, 0)
    for d in range(members):
        start = d * share
        packed = turned_ref[start : start + 8, :]
        for g in range(1, share // 8):
            packed = packed + pltpu.roll(turned_ref[start + 8 * g : start + 8 * g + 8, :], rows * g, 1)
        out_ref[d] = packed.astype(out_ref.dtype)


def kernel_grad(info, x, dh, gb, which, members, dtype, limit=16 << 20):
    frames, width = x.shape
    blocks = width // LANES
    return pl.pallas_call(
        functools.partial(kernel_grad_kernel, ROWS),
        grid_spec=pltpu.PrefetchScalarGridSpec(
            num_scalar_prefetch=1,
            grid=(1,),
            in_specs=[
                pl.BlockSpec((frames, width), lambda i, s: (0, 0)),
                pl.BlockSpec((1, blocks, frames, LANES), lambda i, s: (s[which], 0, 0, 0)),
                pl.BlockSpec((1, 8, width), lambda i, s: (s[which], 0, 0)),
            ],
            out_specs=pl.BlockSpec((members, 8, LANES), lambda i, s: (0, 0, 0)),
            scratch_shapes=[pltpu.VMEM((blocks, PADDED, LANES), F32), pltpu.VMEM((width, LANES), F32)],
        ),
        out_shape=jax.ShapeDtypeStruct((members, 8, LANES), dtype),
        compiler_params=pltpu.CompilerParams(vmem_limit_bytes=limit),
        cost_estimate=pl.CostEstimate(flops=frames * width * 62, bytes_accessed=2 << 20, transcendentals=0),
        name="kernel_grad",
    )(info, x, dh, gb)


def finish_kernel(rows, parts_ref, kernel_ref, gain_ref, bias_ref):
    share = kernel_ref.shape[0]
    total = jnp.sum(parts_ref[...].astype(F32), 0)
    pieces = [total] + [pltpu.roll(total, LANES - rows * g, 1) for g in range(1, share // 8)]
    value = jnp.concatenate(pieces + [jnp.zeros((LANES - share, LANES), F32)], 0)
    kernel_ref[...] = value[:share, :KW]
    turned = value.T
    gain_ref[...] = turned[KW : KW + 1, :share]
    bias_ref[...] = turned[KW + 1 : KW + 2, :share]


def finish(parts, share, limit=8 << 20):
    return pl.pallas_call(
        functools.partial(finish_kernel, ROWS),
        out_shape=[
            jax.ShapeDtypeStruct((share, KW), F32),
            jax.ShapeDtypeStruct((1, share), F32),
            jax.ShapeDtypeStruct((1, share), F32),
        ],
        in_specs=[VMEM],
        out_specs=[VMEM, VMEM, VMEM],
        compiler_params=pltpu.CompilerParams(vmem_limit_bytes=limit),
        name="finish",
    )(parts)


def local(saved, out_grad, lengths, kernel, gain, bias):
    sections = lax.axis_size("pipe")
    members = lax.axis_size("dp")
    place = lax.axis_index("pipe")
    upper = place % 2
    item = 1 - upper
    stages = sections // 2
    stage = stages - 1 - place // 2
    swap = [(p, p ^ 1) for p in range(sections)]
    x_both = saved[0, :, 0]
    x_give = lax.dynamic_index_in_dim(x_both, 1 - item, 0, keepdims=False)
    x_local = lax.dynamic_index_in_dim(x_both, item, 0, keepdims=False)
    w_local = jnp.concatenate([kernel[0].astype(F32), gain, bias], 0)
    w_other = lax.ppermute(w_local, "pipe", swap)
    x_other = lax.ppermute(x_give, "pipe", swap)
    dys = [lax.dynamic_index_in_dim(out_grad[:, 0], item, 0, keepdims=False)]
    length = lax.dynamic_index_in_dim(lengths[:, 0], item, 0, keepdims=False)
    info = jnp.stack([length, stage, upper, 1 - upper, upper]).astype(jnp.int32)
    s_local = forward(info, x_local, w_local)
    s_other = forward(info, x_other, w_other)
    for k in range(stages - 1):
        (dx,) = phase(info, dys, s_local, s_other, w_local, w_other, False)
        top = sections - 1 - 2 * k
        dys.append(lax.ppermute(dx, "pipe", [(top, top - 2), (top - 1, top - 3)]))
    own, give, gb, dh = phase(info, dys, s_local, s_other, w_local, w_other, True)
    kg_give = kernel_grad(info, x_other, dh, gb, 4, members, BF16)
    kg_other = lax.ppermute(kg_give, "pipe", swap)
    kg_own = kernel_grad(info, x_local, dh, gb, 3, members, F32)
    packed = (kg_own + kg_other.astype(F32)).astype(BF16)
    parts = lax.all_to_all(packed, "dp", 0, 0, tiled=True)
    dx_other = lax.ppermute(give, "pipe", swap)
    kernel_part, gain_part, bias_part = finish(parts, kernel.shape[2] // members)
    grads = jnp.where(item == 0, jnp.stack([own, dx_other]), jnp.stack([dx_other, own]))
    return (grads[None, :, None], kernel_part.T[None], gain_part, bias_part)


def solution(mesh):
    return jax.shard_map(
        local,
        mesh=mesh,
        in_specs=(
            P("pipe", None, "dp", None, None),
            P(None, "dp", None, None),
            P(None, "dp"),
            P("pipe", None, None),
            P("pipe", None),
            P("pipe", None),
        ),
        out_specs=(
            P("pipe", None, "dp", None, None),
            P("pipe", None, "dp"),
            P("pipe", "dp"),
            P("pipe", "dp"),
        ),
        check_vma=False,
    )
```

```python
import functools
import jax
import jax.numpy as jnp
from jax import lax
from jax.experimental import pallas as pl
from jax.experimental.pallas import tpu as pltpu
from jax.sharding import PartitionSpec as P


KW = 31
HALF = 15
LANES = 128
LEAD = 16
PADDED = 160
EPS = 1e-05
ROWS = 40
TABLE = 48
F32 = jnp.float32
BF16 = jnp.bfloat16
VMEM = pl.BlockSpec(memory_space=pltpu.VMEM)
SMEM = pl.BlockSpec(memory_space=pltpu.SMEM)
ANY = pl.BlockSpec(memory_space=pl.ANY)


def columns(block):
    return pl.ds(pl.multiple_of(block * LANES, LANES), LANES)


def row_mean(partial, width):
    return jnp.broadcast_to(jnp.sum(partial, 1, keepdims=True) * (1.0 / width), partial.shape)


def live(length, frames):
    return lax.broadcasted_iota(jnp.int32, (frames, LANES), 0) < length


def clear_margins(pad_ref, frames):
    pad_ref[:, 0:LEAD, :] = jnp.zeros((pad_ref.shape[0], LEAD, LANES), F32)
    tail = PADDED - LEAD - frames
    pad_ref[:, LEAD + frames :, :] = jnp.zeros((pad_ref.shape[0], tail, LANES), F32)


def upper_of(place_ref):
    return lax.rem(place_ref[0], 2)


def thirds(value):
    high = value.astype(BF16).astype(F32)
    middle = (value - high).astype(BF16).astype(F32)
    return [high, middle, value - high - middle]


def message_kernel(place_ref, x_ref, kernel_ref, gain_ref, bias_ref, message_ref, w_ref):
    frames, width = x_ref.shape[1:]
    filler = jnp.zeros((TABLE - KW - 6, LANES), F32)

    def copy(b, carry):
        cols = columns(b)
        message_ref[:frames, cols] = x_ref[0, :, cols]
        kernel = kernel_ref[:, cols].astype(F32)
        gain, bias = gain_ref[:, cols], bias_ref[:, cols]
        table = jnp.concatenate([kernel] + thirds(gain) + thirds(bias) + [filler], 0)
        message_ref[frames:, cols] = table.astype(BF16)
        w_ref[:, cols] = jnp.concatenate([kernel, gain, bias], 0)
        return carry

    lax.fori_loop(0, width // LANES, copy, 0)


def whole(*shape):
    return pl.BlockSpec(shape, lambda i, *s: (0,) * len(shape))


def message(place, saved, kernel, gain, bias, limit=8 << 20):
    frames, width = saved.shape[1:]
    return pl.pallas_call(
        message_kernel,
        grid_spec=pltpu.PrefetchScalarGridSpec(
            num_scalar_prefetch=1,
            grid=(1,),
            in_specs=[
                pl.BlockSpec((1, frames, width), lambda i, p: (lax.rem(p[0], 2), 0, 0)),
                whole(KW, width),
                whole(1, width),
                whole(1, width),
            ],
            out_specs=[whole(frames + TABLE, width), whole(KW + 2, width)],
        ),
        out_shape=[
            jax.ShapeDtypeStruct((frames + TABLE, width), BF16),
            jax.ShapeDtypeStruct((KW + 2, width), F32),
        ],
        compiler_params=pltpu.CompilerParams(vmem_limit_bytes=limit),
        cost_estimate=pl.CostEstimate(flops=width * 400, bytes_accessed=1 << 20, transcendentals=0),
        name="message",
    )(place, saved, kernel, gain, bias)


def decode(table_ref, w_ref):
    frames = table_ref.shape[0] - TABLE

    def expand(b, carry):
        cols = columns(b)
        table = table_ref[frames:, cols].astype(F32)
        gain = table[KW : KW + 1] + table[KW + 1 : KW + 2] + table[KW + 2 : KW + 3]
        bias = table[KW + 3 : KW + 4] + table[KW + 4 : KW + 5] + table[KW + 5 : KW + 6]
        w_ref[:, cols] = jnp.concatenate([table[:KW], gain, bias], 0)
        return carry

    lax.fori_loop(0, table_ref.shape[1] // LANES, expand, 0)


def forward_local_kernel(place_ref, lens_ref, x_ref, w_ref, s_ref, pad_ref):
    forward_body(lens_ref[1 - upper_of(place_ref)], x_ref.at[0], w_ref, s_ref, pad_ref)


def forward_other_kernel(place_ref, lens_ref, message_ref, s_ref, w_ref, pad_ref):
    frames = message_ref.shape[0] - TABLE
    decode(message_ref, w_ref)
    forward_body(lens_ref[1 - upper_of(place_ref)], message_ref.at[pl.ds(0, frames)], w_ref, s_ref, pad_ref)


def forward_body(length, x_ref, w_ref, s_ref, pad_ref):
    frames, width = x_ref.shape
    blocks = width // LANES
    mask = live(length, frames)
    clear_margins(pad_ref, frames)
    zero = jnp.zeros((frames, LANES), F32)

    def convolve(b, total):
        cols = columns(b)
        pad_ref[b, LEAD : LEAD + frames, :] = jnp.where(mask, x_ref[:, cols].astype(F32), 0.0)
        h = zero
        for j in range(KW):
            h = h + w_ref[j : j + 1, cols] * pad_ref[b, LEAD - HALF + j : LEAD - HALF + j + frames, :]
        s_ref[b] = h
        return total + h

    mu = row_mean(lax.fori_loop(0, blocks, convolve, zero), width)

    def square(b, total):
        centred = s_ref[b] - mu
        return total + centred * centred

    recip = lax.rsqrt(row_mean(lax.fori_loop(0, blocks, square, zero), width) + EPS)
    s_ref[2 * blocks] = recip

    def activate(b, carry):
        cols = columns(b)
        normed = (s_ref[b] - mu) * recip
        u = normed * w_ref[KW : KW + 1, cols] + w_ref[KW + 1 : KW + 2, cols]
        sig = jax.nn.sigmoid(u)
        s_ref[b] = normed
        s_ref[blocks + b] = jnp.where(mask, sig * (1.0 + u * (1.0 - sig)), 0.0)
        return carry

    lax.fori_loop(0, blocks, activate, 0)


def forward(place, lens, x, w, limit=16 << 20):
    frames, width = (x.shape[0] - TABLE, x.shape[1]) if w is None else x.shape[1:]
    blocks = width // LANES
    stats = (2 * blocks + 1, frames, LANES)
    if w is None:
        body, operands = forward_other_kernel, (x,)
        in_specs = [whole(frames + TABLE, width)]
        out_specs = [whole(*stats), whole(KW + 2, width)]
        out_shape = [jax.ShapeDtypeStruct(stats, F32), jax.ShapeDtypeStruct((KW + 2, width), F32)]
    else:
        body, operands = forward_local_kernel, (x, w)
        in_specs = [
            pl.BlockSpec((1, frames, width), lambda i, p, n: (1 - lax.rem(p[0], 2), 0, 0)),
            whole(KW + 2, width),
        ]
        out_specs = whole(*stats)
        out_shape = jax.ShapeDtypeStruct(stats, F32)
    return pl.pallas_call(
        body,
        grid_spec=pltpu.PrefetchScalarGridSpec(
            num_scalar_prefetch=2,
            grid=(1,),
            in_specs=in_specs,
            out_specs=out_specs,
            scratch_shapes=[pltpu.VMEM((blocks, PADDED, LANES), F32)],
        ),
        out_shape=out_shape,
        compiler_params=pltpu.CompilerParams(vmem_limit_bytes=limit),
        cost_estimate=pl.CostEstimate(flops=frames * width * 100, bytes_accessed=3 << 20, transcendentals=frames * width),
        name="forward_other" if w is None else "forward_local",
    )(place, lens, *operands)


def section(i, mask, dy_ref, s_ref, w_ref, pad_ref, dx_ref, gb_ref, dh_ref):
    frames, width = dy_ref.shape
    blocks = width // LANES
    zero = jnp.zeros((frames, LANES), F32)

    def scale(b, totals):
        first, second = totals
        cols = columns(b)
        normed = s_ref[i, b]
        du = dy_ref[:, cols].astype(F32) * s_ref[i, blocks + b]
        dnorm = du * w_ref[i, KW : KW + 1, cols]
        pad_ref[b, LEAD : LEAD + frames, :] = dnorm
        if gb_ref is not None:
            gb_ref[i, 0:1, cols] = jnp.sum(du * normed, 0, keepdims=True)
            gb_ref[i, 1:2, cols] = jnp.sum(du, 0, keepdims=True)
        return first + dnorm, second + dnorm * normed

    first, second = lax.fori_loop(0, blocks, scale, (zero, zero))
    first, second = row_mean(first, width), row_mean(second, width)

    def convolve(b, carry):
        cols = columns(b)
        dh = s_ref[i, 2 * blocks] * (pad_ref[b, LEAD : LEAD + frames, :] - first - s_ref[i, b] * second)
        pad_ref[b, LEAD : LEAD + frames, :] = dh
        if dh_ref is not None:
            dh_ref[i, b] = dh
        back = dy_ref[:, cols].astype(F32)
        for j in range(KW):
            start = LEAD + HALF - j
            back = back + w_ref[i, j : j + 1, cols] * pad_ref[b, start : start + frames, :]
        dx_ref[:, cols] = jnp.where(mask, back, 0.0).astype(BF16)
        return carry

    lax.fori_loop(0, blocks, convolve, 0)


def phase_kernel(n_dy, last, stages, place_ref, lens_ref, *refs):
    dys = refs[:n_dy]
    s_local, s_other, w_local, w_other = refs[n_dy : n_dy + 4]
    refs = refs[n_dy + 4 :]
    if last:
        own_ref, give_ref, gb_ref, dh_ref = refs[:4]
        dy_ref, first_ref, s_ref, w_ref, pad_ref, sem, dx_ref = refs[4:]
    else:
        dx_ref = refs[0]
        dy_ref, first_ref, s_ref, w_ref, pad_ref, sem = refs[1:]
        gb_ref = dh_ref = None
    local_first = upper_of(place_ref)
    item = 1 - local_first
    length = lens_ref[item]
    stage = stages - 1 - lax.div(place_ref[0], 2)
    frames = dy_ref.shape[0]

    def fetch(a, b):
        return [
            pltpu.make_async_copy(a[0], w_ref.at[0], sem.at[1]),
            pltpu.make_async_copy(a[1], s_ref.at[0], sem.at[2]),
            pltpu.make_async_copy(b[0], w_ref.at[1], sem.at[3]),
            pltpu.make_async_copy(b[1], s_ref.at[1], sem.at[4]),
        ]

    chosen = jnp.minimum(stage, n_dy - 1)
    for k in range(n_dy):

        @pl.when(chosen == k)
        def _():
            pltpu.make_async_copy(dys[k] if k else dys[k].at[item], dy_ref, sem.at[0]).start()

    ahead = fetch((w_local, s_local), (w_other, s_other))
    behind = fetch((w_other, s_other), (w_local, s_local))

    @pl.when(local_first == 1)
    def _():
        for copy in ahead:
            copy.start()

    @pl.when(local_first != 1)
    def _():
        for copy in behind:
            copy.start()

    clear_margins(pad_ref, frames)
    mask = live(length, frames)
    pltpu.make_async_copy(dys[0].at[item], dy_ref, sem.at[0]).wait()
    ahead[0].wait()
    ahead[1].wait()
    section(0, mask, dy_ref, s_ref, w_ref, pad_ref, first_ref, gb_ref, dh_ref)
    ahead[2].wait()
    ahead[3].wait()
    section(1, mask, first_ref, s_ref, w_ref, pad_ref, dx_ref, gb_ref, dh_ref)
    if last:

        @pl.when(local_first == 1)
        def _():
            own_ref[...] = first_ref[...]
            give_ref[...] = dx_ref[...]

        @pl.when(local_first != 1)
        def _():
            own_ref[...] = dx_ref[...]
            give_ref[...] = first_ref[...]


def phase(place, lens, stages, dys, s_local, s_other, w_local, w_other, last, limit=20 << 20):
    frames, width = dys[0].shape[1:]
    blocks = width // LANES
    dx = jax.ShapeDtypeStruct((frames, width), BF16)
    out_shape = [dx]
    scratch = [
        pltpu.VMEM((frames, width), BF16),
        pltpu.VMEM((frames, width), BF16),
        pltpu.VMEM((2,) + s_local.shape, F32),
        pltpu.VMEM((2,) + w_local.shape, F32),
        pltpu.VMEM((blocks, PADDED, LANES), F32),
        pltpu.SemaphoreType.DMA((5,)),
    ]
    if last:
        out_shape = [
            dx,
            dx,
            jax.ShapeDtypeStruct((2, 8, width), F32),
            jax.ShapeDtypeStruct((2, blocks, frames, LANES), F32),
        ]
        scratch.append(pltpu.VMEM((frames, width), BF16))
    return pl.pallas_call(
        functools.partial(phase_kernel, len(dys), last, stages),
        out_shape=out_shape,
        in_specs=[SMEM, SMEM] + [ANY] * (len(dys) + 4),
        out_specs=[VMEM] * len(out_shape),
        scratch_shapes=scratch,
        compiler_params=pltpu.CompilerParams(vmem_limit_bytes=limit),
        cost_estimate=pl.CostEstimate(flops=frames * width * 160, bytes_accessed=5 << 20, transcendentals=0),
        name="phase_last" if last else "phase",
    )(place, lens, *dys, s_local, s_other, w_local, w_other)


def kernel_grad_kernel(place_ref, lens_ref, x_ref, dh_ref, gb_ref, out_ref, pad_ref):
    frames = dh_ref.shape[2]
    blocks = dh_ref.shape[1]
    mask = live(lens_ref[1 - upper_of(place_ref)], frames)
    clear_margins(pad_ref, frames)
    filler = jnp.zeros((ROWS - KW - 2, LANES), F32)

    def correlate(b, carry):
        cols = columns(b)
        x = x_ref[:frames, cols] if len(x_ref.shape) == 2 else x_ref[0, :, cols]
        pad_ref[b, LEAD : LEAD + frames, :] = jnp.where(mask, x.astype(F32), 0.0)
        dh = dh_ref[0, b]
        sums = []
        for j in range(KW):
            product = dh * pad_ref[b, LEAD - HALF + j : LEAD - HALF + j + frames, :]
            sums.append(jnp.sum(product, 0, keepdims=True))
        sums.append(gb_ref[0, 0:1, cols])
        sums.append(gb_ref[0, 1:2, cols])
        out_ref[:, cols] = jnp.concatenate(sums + [filler], 0).astype(out_ref.dtype)
        return carry

    lax.fori_loop(0, blocks, correlate, 0)


def kernel_grad(place, lens, x, dh, gb, own, limit=16 << 20):
    blocks, frames = dh.shape[1:3]
    width = blocks * LANES
    if own:
        x_spec = pl.BlockSpec((1, frames, width), lambda i, p, n: (1 - lax.rem(p[0], 2), 0, 0))
        which = lambda p: 1 - lax.rem(p[0], 2)
    else:
        x_spec = whole(*x.shape)
        which = lambda p: lax.rem(p[0], 2)
    return pl.pallas_call(
        kernel_grad_kernel,
        grid_spec=pltpu.PrefetchScalarGridSpec(
            num_scalar_prefetch=2,
            grid=(1,),
            in_specs=[
                x_spec,
                pl.BlockSpec((1, blocks, frames, LANES), lambda i, p, n: (which(p), 0, 0, 0)),
                pl.BlockSpec((1, 8, width), lambda i, p, n: (which(p), 0, 0)),
            ],
            out_specs=whole(ROWS, width),
            scratch_shapes=[pltpu.VMEM((blocks, PADDED, LANES), F32)],
        ),
        out_shape=jax.ShapeDtypeStruct((ROWS, width), F32 if own else BF16),
        compiler_params=pltpu.CompilerParams(vmem_limit_bytes=limit),
        cost_estimate=pl.CostEstimate(flops=frames * width * 62, bytes_accessed=2 << 20, transcendentals=0),
        name="kernel_grad_own" if own else "kernel_grad_other",
    )(place, lens, x, dh, gb)


def pack_kernel(own_ref, other_ref, out_ref, turned_ref):
    rows, width = own_ref.shape
    members = out_ref.shape[0]
    share = width // members
    filler = jnp.zeros((LANES - rows, LANES), F32)
    for b in range(width // LANES):
        cols = pl.ds(b * LANES, LANES)
        total = own_ref[:, cols] + other_ref[:, cols].astype(F32)
        turned_ref[cols, :] = jnp.concatenate([total, filler], 0).T
    for d in range(members):
        start = d * share
        packed = turned_ref[start : start + 8, :]
        for g in range(1, share // 8):
            packed = packed + pltpu.roll(turned_ref[start + 8 * g : start + 8 * g + 8, :], rows * g, 1)
        out_ref[d] = packed.astype(out_ref.dtype)


def pack(own, other, members, limit=8 << 20):
    width = own.shape[1]
    return pl.pallas_call(
        pack_kernel,
        out_shape=jax.ShapeDtypeStruct((members, 8, LANES), BF16),
        in_specs=[VMEM, VMEM],
        out_specs=VMEM,
        scratch_shapes=[pltpu.VMEM((width, LANES), F32)],
        compiler_params=pltpu.CompilerParams(vmem_limit_bytes=limit),
        cost_estimate=pl.CostEstimate(flops=width * 256, bytes_accessed=1 << 19, transcendentals=0),
        name="pack",
    )(own, other)


def finish_kernel(rows, parts_ref, kernel_ref, gain_ref, bias_ref):
    share = kernel_ref.shape[0]
    total = jnp.sum(parts_ref[...].astype(F32), 0)
    pieces = [total] + [pltpu.roll(total, LANES - rows * g, 1) for g in range(1, share // 8)]
    value = jnp.concatenate(pieces + [jnp.zeros((LANES - share, LANES), F32)], 0)
    kernel_ref[...] = value[:share, :KW]
    turned = value.T
    gain_ref[...] = turned[KW : KW + 1, :share]
    bias_ref[...] = turned[KW + 1 : KW + 2, :share]


def finish(parts, share, limit=8 << 20):
    return pl.pallas_call(
        functools.partial(finish_kernel, ROWS),
        out_shape=[
            jax.ShapeDtypeStruct((share, KW), F32),
            jax.ShapeDtypeStruct((1, share), F32),
            jax.ShapeDtypeStruct((1, share), F32),
        ],
        in_specs=[VMEM],
        out_specs=[VMEM, VMEM, VMEM],
        compiler_params=pltpu.CompilerParams(vmem_limit_bytes=limit),
        name="finish",
    )(parts)


def local(saved, out_grad, lengths, kernel, gain, bias):
    sections = lax.axis_size("pipe")
    members = lax.axis_size("dp")
    place = lax.axis_index("pipe").astype(jnp.int32)
    item = 1 - place % 2
    place = jnp.reshape(place, (1,))
    lens = lengths[:, 0]
    stages = sections // 2
    swap = [(p, p ^ 1) for p in range(sections)]
    saved = saved[0, :, 0]
    sent, w_local = message(place, saved, kernel[0], gain, bias)
    came = lax.ppermute(sent, "pipe", swap)
    dys = [out_grad[:, 0]]
    s_local = forward(place, lens, saved, w_local)
    s_other, w_other = forward(place, lens, came, None)
    for k in range(stages - 1):
        (dx,) = phase(place, lens, stages, dys, s_local, s_other, w_local, w_other, False)
        top = sections - 1 - 2 * k
        dys.append(lax.ppermute(dx, "pipe", [(top, top - 2), (top - 1, top - 3)]))
    own, give, gb, dh = phase(place, lens, stages, dys, s_local, s_other, w_local, w_other, True)
    kg_give = kernel_grad(place, lens, came, dh, gb, False)
    kg_other = lax.ppermute(kg_give, "pipe", swap)
    kg_own = kernel_grad(place, lens, saved, dh, gb, True)
    packed = pack(kg_own, kg_other, members)
    parts = lax.all_to_all(packed, "dp", 0, 0, tiled=True)
    dx_other = lax.ppermute(give, "pipe", swap)
    kernel_part, gain_part, bias_part = finish(parts, kernel.shape[2] // members)
    grads = jnp.where(item == 0, jnp.stack([own, dx_other]), jnp.stack([dx_other, own]))
    return (grads[None, :, None], kernel_part.T[None], gain_part, bias_part)


def solution(mesh):
    return jax.shard_map(
        local,
        mesh=mesh,
        in_specs=(
            P("pipe", None, "dp", None, None),
            P(None, "dp", None, None),
            P(None, "dp"),
            P("pipe", None, None),
            P("pipe", None),
            P("pipe", None),
        ),
        out_specs=(
            P("pipe", None, "dp", None, None),
            P("pipe", None, "dp"),
            P("pipe", "dp"),
            P("pipe", "dp"),
        ),
        check_vma=False,
    )
```

```python
import functools
import jax
import jax.numpy as jnp
from jax import lax
from jax.experimental import pallas as pl
from jax.experimental.pallas import tpu as pltpu
from jax.sharding import PartitionSpec as P


KW = 31
HALF = 15
LANES = 128
LEAD = 16
PADDED = 160
EPS = 1e-05
ROWS = 40
TABLE = 40
F32 = jnp.float32
BF16 = jnp.bfloat16
VMEM = pl.BlockSpec(memory_space=pltpu.VMEM)
SMEM = pl.BlockSpec(memory_space=pltpu.SMEM)
ANY = pl.BlockSpec(memory_space=pl.ANY)
HBM = pl.BlockSpec(memory_space=pltpu.HBM)


def columns(block):
    return pl.ds(pl.multiple_of(block * LANES, LANES), LANES)


def row_mean(partial, width):
    return jnp.broadcast_to(jnp.sum(partial, 1, keepdims=True) * (1.0 / width), partial.shape)


def live(length, frames):
    return lax.broadcasted_iota(jnp.int32, (frames, LANES), 0) < length


def clear_margins(pad_ref, frames):
    pad_ref[:, 0:LEAD, :] = jnp.zeros((pad_ref.shape[0], LEAD, LANES), F32)
    tail = PADDED - LEAD - frames
    pad_ref[:, LEAD + frames :, :] = jnp.zeros((pad_ref.shape[0], tail, LANES), F32)


def upper_of(place_ref):
    return lax.rem(place_ref[0], 2)


def thirds(value):
    high = value.astype(BF16).astype(F32)
    middle = (value - high).astype(BF16).astype(F32)
    return [high, middle, value - high - middle]


def message_kernel(place_ref, saved_hbm, kernel_hbm, gain_hbm, bias_hbm, message_ref, w_ref, x_ref, kernel_ref, gain_ref, bias_ref, sem):
    frames, width = x_ref.shape
    filler = jnp.zeros((TABLE - KW - 6, LANES), F32)
    upper = upper_of(place_ref)
    copies = [
        pltpu.make_async_copy(kernel_hbm, kernel_ref, sem.at[0]),
        pltpu.make_async_copy(gain_hbm, gain_ref, sem.at[1]),
        pltpu.make_async_copy(bias_hbm, bias_ref, sem.at[2]),
        pltpu.make_async_copy(saved_hbm.at[upper], message_ref.at[pl.ds(0, frames)], sem.at[3]),
        pltpu.make_async_copy(saved_hbm.at[1 - upper], x_ref, sem.at[4]),
    ]
    for copy in copies:
        copy.start()
    for copy in copies[:3]:
        copy.wait()

    def tabulate(b, carry):
        cols = columns(b)
        kernel = kernel_ref[:, cols].astype(F32)
        gain, bias = gain_ref[:, cols], bias_ref[:, cols]
        table = jnp.concatenate([kernel] + thirds(gain) + thirds(bias) + [filler], 0)
        message_ref[frames:, cols] = table.astype(BF16)
        w_ref[:, cols] = jnp.concatenate([kernel, gain, bias], 0)
        return carry

    lax.fori_loop(0, width // LANES, tabulate, 0)
    for copy in copies[3:]:
        copy.wait()


def whole(*shape):
    return pl.BlockSpec(shape, lambda i, *s: (0,) * len(shape))


def message(place, saved, kernel, gain, bias, limit=8 << 20):
    frames, width = saved.shape[1:]
    return pl.pallas_call(
        message_kernel,
        in_specs=[SMEM, HBM, HBM, HBM, HBM],
        out_specs=[VMEM, VMEM, VMEM],
        out_shape=[
            jax.ShapeDtypeStruct((frames + TABLE, width), BF16),
            jax.ShapeDtypeStruct((KW + 2, width), F32),
            jax.ShapeDtypeStruct((frames, width), BF16),
        ],
        scratch_shapes=[
            pltpu.VMEM((KW, width), BF16),
            pltpu.VMEM((1, width), F32),
            pltpu.VMEM((1, width), F32),
            pltpu.SemaphoreType.DMA((5,)),
        ],
        compiler_params=pltpu.CompilerParams(vmem_limit_bytes=limit),
        cost_estimate=pl.CostEstimate(flops=width * 400, bytes_accessed=1 << 20, transcendentals=0),
        name="message",
    )(place, saved, kernel, gain, bias)


def decode(table_ref, w_ref):
    frames = table_ref.shape[0] - TABLE

    def expand(b, carry):
        cols = columns(b)
        table = table_ref[frames:, cols].astype(F32)
        gain = table[KW : KW + 1] + table[KW + 1 : KW + 2] + table[KW + 2 : KW + 3]
        bias = table[KW + 3 : KW + 4] + table[KW + 4 : KW + 5] + table[KW + 5 : KW + 6]
        w_ref[:, cols] = jnp.concatenate([table[:KW], gain, bias], 0)
        return carry

    lax.fori_loop(0, table_ref.shape[1] // LANES, expand, 0)


def forward_local_kernel(place_ref, lens_ref, x_ref, w_ref, s_ref, pad_ref):
    forward_body(lens_ref[1 - upper_of(place_ref)], x_ref, w_ref, s_ref, pad_ref)


def forward_other_kernel(place_ref, lens_ref, message_ref, s_ref, w_ref, pad_ref):
    frames = message_ref.shape[0] - TABLE
    decode(message_ref, w_ref)
    forward_body(lens_ref[1 - upper_of(place_ref)], message_ref.at[pl.ds(0, frames)], w_ref, s_ref, pad_ref)


def forward_body(length, x_ref, w_ref, s_ref, pad_ref):
    frames, width = x_ref.shape
    blocks = width // LANES
    mask = live(length, frames)
    clear_margins(pad_ref, frames)
    zero = jnp.zeros((frames, LANES), F32)

    def convolve(b, total):
        cols = columns(b)
        pad_ref[b, LEAD : LEAD + frames, :] = jnp.where(mask, x_ref[:, cols].astype(F32), 0.0)
        h = zero
        for j in range(KW):
            h = h + w_ref[j : j + 1, cols] * pad_ref[b, LEAD - HALF + j : LEAD - HALF + j + frames, :]
        s_ref[b] = h
        return total + h

    mu = row_mean(lax.fori_loop(0, blocks, convolve, zero), width)

    def square(b, total):
        centred = s_ref[b] - mu
        return total + centred * centred

    recip = lax.rsqrt(row_mean(lax.fori_loop(0, blocks, square, zero), width) + EPS)
    s_ref[2 * blocks] = recip

    def activate(b, carry):
        cols = columns(b)
        normed = (s_ref[b] - mu) * recip
        u = normed * w_ref[KW : KW + 1, cols] + w_ref[KW + 1 : KW + 2, cols]
        sig = jax.nn.sigmoid(u)
        s_ref[b] = normed
        s_ref[blocks + b] = jnp.where(mask, sig * (1.0 + u * (1.0 - sig)), 0.0)
        return carry

    lax.fori_loop(0, blocks, activate, 0)


def forward(place, lens, x, w, limit=16 << 20):
    frames, width = (x.shape[0] - TABLE, x.shape[1]) if w is None else x.shape
    blocks = width // LANES
    stats = (2 * blocks + 1, frames, LANES)
    if w is None:
        body, operands = forward_other_kernel, (x,)
        in_specs = [whole(frames + TABLE, width)]
        out_specs = [whole(*stats), whole(KW + 2, width)]
        out_shape = [jax.ShapeDtypeStruct(stats, F32), jax.ShapeDtypeStruct((KW + 2, width), F32)]
    else:
        body, operands = forward_local_kernel, (x, w)
        in_specs = [whole(frames, width), whole(KW + 2, width)]
        out_specs = whole(*stats)
        out_shape = jax.ShapeDtypeStruct(stats, F32)
    return pl.pallas_call(
        body,
        grid_spec=pltpu.PrefetchScalarGridSpec(
            num_scalar_prefetch=2,
            grid=(1,),
            in_specs=in_specs,
            out_specs=out_specs,
            scratch_shapes=[pltpu.VMEM((blocks, PADDED, LANES), F32)],
        ),
        out_shape=out_shape,
        compiler_params=pltpu.CompilerParams(vmem_limit_bytes=limit),
        cost_estimate=pl.CostEstimate(flops=frames * width * 100, bytes_accessed=3 << 20, transcendentals=frames * width),
        name="forward_other" if w is None else "forward_local",
    )(place, lens, *operands)


def section(i, mask, dy_ref, s_ref, w_ref, pad_ref, dx_ref, gb_ref, dh_ref):
    frames, width = dy_ref.shape
    blocks = width // LANES
    zero = jnp.zeros((frames, LANES), F32)

    def scale(b, totals):
        first, second = totals
        cols = columns(b)
        normed = s_ref[i, b]
        du = dy_ref[:, cols].astype(F32) * s_ref[i, blocks + b]
        dnorm = du * w_ref[i, KW : KW + 1, cols]
        pad_ref[b, LEAD : LEAD + frames, :] = dnorm
        if gb_ref is not None:
            gb_ref[i, 0:1, cols] = jnp.sum(du * normed, 0, keepdims=True)
            gb_ref[i, 1:2, cols] = jnp.sum(du, 0, keepdims=True)
        return first + dnorm, second + dnorm * normed

    first, second = lax.fori_loop(0, blocks, scale, (zero, zero))
    first, second = row_mean(first, width), row_mean(second, width)

    def convolve(b, carry):
        cols = columns(b)
        dh = s_ref[i, 2 * blocks] * (pad_ref[b, LEAD : LEAD + frames, :] - first - s_ref[i, b] * second)
        pad_ref[b, LEAD : LEAD + frames, :] = dh
        if dh_ref is not None:
            dh_ref[i, b] = dh
        back = dy_ref[:, cols].astype(F32)
        for j in range(KW):
            start = LEAD + HALF - j
            back = back + w_ref[i, j : j + 1, cols] * pad_ref[b, start : start + frames, :]
        dx_ref[:, cols] = jnp.where(mask, back, 0.0).astype(BF16)
        return carry

    lax.fori_loop(0, blocks, convolve, 0)


def phase_kernel(n_dy, last, stages, place_ref, lens_ref, *refs):
    dys = refs[:n_dy]
    s_local, s_other, w_local, w_other = refs[n_dy : n_dy + 4]
    refs = refs[n_dy + 4 :]
    if last:
        own_ref, give_ref, gb_ref, dh_ref = refs[:4]
        dy_ref, first_ref, s_ref, w_ref, pad_ref, sem, dx_ref = refs[4:]
    else:
        dx_ref = refs[0]
        dy_ref, first_ref, s_ref, w_ref, pad_ref, sem = refs[1:]
        gb_ref = dh_ref = None
    local_first = upper_of(place_ref)
    item = 1 - local_first
    length = lens_ref[item]
    stage = stages - 1 - lax.div(place_ref[0], 2)
    frames = dy_ref.shape[0]

    def fetch(a, b):
        return [
            pltpu.make_async_copy(a[0], w_ref.at[0], sem.at[1]),
            pltpu.make_async_copy(a[1], s_ref.at[0], sem.at[2]),
            pltpu.make_async_copy(b[0], w_ref.at[1], sem.at[3]),
            pltpu.make_async_copy(b[1], s_ref.at[1], sem.at[4]),
        ]

    chosen = jnp.minimum(stage, n_dy - 1)
    for k in range(n_dy):

        @pl.when(chosen == k)
        def _():
            pltpu.make_async_copy(dys[k] if k else dys[k].at[item], dy_ref, sem.at[0]).start()

    ahead = fetch((w_local, s_local), (w_other, s_other))
    behind = fetch((w_other, s_other), (w_local, s_local))

    @pl.when(local_first == 1)
    def _():
        for copy in ahead:
            copy.start()

    @pl.when(local_first != 1)
    def _():
        for copy in behind:
            copy.start()

    clear_margins(pad_ref, frames)
    mask = live(length, frames)
    pltpu.make_async_copy(dys[0].at[item], dy_ref, sem.at[0]).wait()
    ahead[0].wait()
    ahead[1].wait()
    section(0, mask, dy_ref, s_ref, w_ref, pad_ref, first_ref, gb_ref, dh_ref)
    ahead[2].wait()
    ahead[3].wait()
    section(1, mask, first_ref, s_ref, w_ref, pad_ref, dx_ref, gb_ref, dh_ref)
    if last:

        @pl.when(local_first == 1)
        def _():
            own_ref[...] = first_ref[...]
            give_ref[...] = dx_ref[...]

        @pl.when(local_first != 1)
        def _():
            own_ref[...] = dx_ref[...]
            give_ref[...] = first_ref[...]


def phase(place, lens, stages, dys, s_local, s_other, w_local, w_other, last, limit=20 << 20):
    frames, width = dys[0].shape[1:]
    blocks = width // LANES
    dx = jax.ShapeDtypeStruct((frames, width), BF16)
    out_shape = [dx]
    scratch = [
        pltpu.VMEM((frames, width), BF16),
        pltpu.VMEM((frames, width), BF16),
        pltpu.VMEM((2,) + s_local.shape, F32),
        pltpu.VMEM((2,) + w_local.shape, F32),
        pltpu.VMEM((blocks, PADDED, LANES), F32),
        pltpu.SemaphoreType.DMA((5,)),
    ]
    if last:
        out_shape = [
            dx,
            dx,
            jax.ShapeDtypeStruct((2, 8, width), F32),
            jax.ShapeDtypeStruct((2, blocks, frames, LANES), F32),
        ]
        scratch.append(pltpu.VMEM((frames, width), BF16))
    return pl.pallas_call(
        functools.partial(phase_kernel, len(dys), last, stages),
        out_shape=out_shape,
        in_specs=[SMEM, SMEM] + [ANY] * (len(dys) + 4),
        out_specs=[VMEM] * len(out_shape),
        scratch_shapes=scratch,
        compiler_params=pltpu.CompilerParams(vmem_limit_bytes=limit),
        cost_estimate=pl.CostEstimate(flops=frames * width * 160, bytes_accessed=5 << 20, transcendentals=0),
        name="phase_last" if last else "phase",
    )(place, lens, *dys, s_local, s_other, w_local, w_other)


def kernel_grad_kernel(place_ref, lens_ref, x_ref, dh_ref, gb_ref, out_ref, pad_ref):
    frames = dh_ref.shape[2]
    blocks = dh_ref.shape[1]
    mask = live(lens_ref[1 - upper_of(place_ref)], frames)
    clear_margins(pad_ref, frames)
    filler = jnp.zeros((ROWS - KW - 2, LANES), F32)

    def correlate(b, carry):
        cols = columns(b)
        pad_ref[b, LEAD : LEAD + frames, :] = jnp.where(mask, x_ref[:frames, cols].astype(F32), 0.0)
        dh = dh_ref[0, b]
        sums = []
        for j in range(KW):
            product = dh * pad_ref[b, LEAD - HALF + j : LEAD - HALF + j + frames, :]
            sums.append(jnp.sum(product, 0, keepdims=True))
        sums.append(gb_ref[0, 0:1, cols])
        sums.append(gb_ref[0, 1:2, cols])
        out_ref[:, cols] = jnp.concatenate(sums + [filler], 0).astype(out_ref.dtype)
        return carry

    lax.fori_loop(0, blocks, correlate, 0)


def kernel_grad(place, lens, x, dh, gb, own, limit=16 << 20):
    blocks, frames = dh.shape[1:3]
    width = blocks * LANES
    if own:
        which = lambda p: 1 - lax.rem(p[0], 2)
    else:
        which = lambda p: lax.rem(p[0], 2)
    return pl.pallas_call(
        kernel_grad_kernel,
        grid_spec=pltpu.PrefetchScalarGridSpec(
            num_scalar_prefetch=2,
            grid=(1,),
            in_specs=[
                whole(*x.shape),
                pl.BlockSpec((1, blocks, frames, LANES), lambda i, p, n: (which(p), 0, 0, 0)),
                pl.BlockSpec((1, 8, width), lambda i, p, n: (which(p), 0, 0)),
            ],
            out_specs=whole(ROWS, width),
            scratch_shapes=[pltpu.VMEM((blocks, PADDED, LANES), F32)],
        ),
        out_shape=jax.ShapeDtypeStruct((ROWS, width), F32 if own else BF16),
        compiler_params=pltpu.CompilerParams(vmem_limit_bytes=limit),
        cost_estimate=pl.CostEstimate(flops=frames * width * 62, bytes_accessed=2 << 20, transcendentals=0),
        name="kernel_grad_own" if own else "kernel_grad_other",
    )(place, lens, x, dh, gb)


def pack_kernel(own_ref, other_ref, out_ref, turned_ref):
    rows, width = own_ref.shape
    members = out_ref.shape[0]
    share = width // members
    filler = jnp.zeros((LANES - rows, LANES), F32)
    for b in range(width // LANES):
        cols = pl.ds(b * LANES, LANES)
        total = own_ref[:, cols] + other_ref[:, cols].astype(F32)
        turned_ref[cols, :] = jnp.concatenate([total, filler], 0).T
    for d in range(members):
        start = d * share
        packed = turned_ref[start : start + 8, :]
        for g in range(1, share // 8):
            packed = packed + pltpu.roll(turned_ref[start + 8 * g : start + 8 * g + 8, :], rows * g, 1)
        out_ref[d] = packed.astype(out_ref.dtype)


def pack(own, other, members, limit=8 << 20):
    width = own.shape[1]
    return pl.pallas_call(
        pack_kernel,
        out_shape=jax.ShapeDtypeStruct((members, 8, LANES), BF16),
        in_specs=[VMEM, VMEM],
        out_specs=VMEM,
        scratch_shapes=[pltpu.VMEM((width, LANES), F32)],
        compiler_params=pltpu.CompilerParams(vmem_limit_bytes=limit),
        cost_estimate=pl.CostEstimate(flops=width * 256, bytes_accessed=1 << 19, transcendentals=0),
        name="pack",
    )(own, other)


def finish_kernel(rows, parts_ref, kernel_ref, gain_ref, bias_ref):
    share = kernel_ref.shape[0]
    total = jnp.sum(parts_ref[...].astype(F32), 0)
    pieces = [total] + [pltpu.roll(total, LANES - rows * g, 1) for g in range(1, share // 8)]
    value = jnp.concatenate(pieces + [jnp.zeros((LANES - share, LANES), F32)], 0)
    kernel_ref[...] = value[:share, :KW]
    turned = value.T
    gain_ref[...] = turned[KW : KW + 1, :share]
    bias_ref[...] = turned[KW + 1 : KW + 2, :share]


def finish(parts, share, limit=8 << 20):
    return pl.pallas_call(
        functools.partial(finish_kernel, ROWS),
        out_shape=[
            jax.ShapeDtypeStruct((share, KW), F32),
            jax.ShapeDtypeStruct((1, share), F32),
            jax.ShapeDtypeStruct((1, share), F32),
        ],
        in_specs=[VMEM],
        out_specs=[VMEM, VMEM, VMEM],
        compiler_params=pltpu.CompilerParams(vmem_limit_bytes=limit),
        name="finish",
    )(parts)


def local(saved, out_grad, lengths, kernel, gain, bias):
    sections = lax.axis_size("pipe")
    members = lax.axis_size("dp")
    place = lax.axis_index("pipe").astype(jnp.int32)
    item = 1 - place % 2
    place = jnp.reshape(place, (1,))
    lens = lengths[:, 0]
    stages = sections // 2
    swap = [(p, p ^ 1) for p in range(sections)]
    sent, w_local, x_local = message(place, saved[0, :, 0], kernel[0], gain, bias)
    came = lax.ppermute(sent, "pipe", swap)
    dys = [out_grad[:, 0]]
    s_local = forward(place, lens, x_local, w_local)
    s_other, w_other = forward(place, lens, came, None)
    for k in range(stages - 1):
        (dx,) = phase(place, lens, stages, dys, s_local, s_other, w_local, w_other, False)
        top = sections - 1 - 2 * k
        dys.append(lax.ppermute(dx, "pipe", [(top, top - 2), (top - 1, top - 3)]))
    own, give, gb, dh = phase(place, lens, stages, dys, s_local, s_other, w_local, w_other, True)
    kg_give = kernel_grad(place, lens, came, dh, gb, False)
    kg_other = lax.ppermute(kg_give, "pipe", swap)
    kg_own = kernel_grad(place, lens, x_local, dh, gb, True)
    packed = pack(kg_own, kg_other, members)
    parts = lax.all_to_all(packed, "dp", 0, 0, tiled=True)
    dx_other = lax.ppermute(give, "pipe", swap)
    kernel_part, gain_part, bias_part = finish(parts, kernel.shape[2] // members)
    grads = jnp.where(item == 0, jnp.stack([own, dx_other]), jnp.stack([dx_other, own]))
    return (grads[None, :, None], kernel_part.T[None], gain_part, bias_part)


def solution(mesh):
    return jax.shard_map(
        local,
        mesh=mesh,
        in_specs=(
            P("pipe", None, "dp", None, None),
            P(None, "dp", None, None),
            P(None, "dp"),
            P("pipe", None, None),
            P("pipe", None),
            P("pipe", None),
        ),
        out_specs=(
            P("pipe", None, "dp", None, None),
            P("pipe", None, "dp"),
            P("pipe", "dp"),
            P("pipe", "dp"),
        ),
        check_vma=False,
    )
```
